256 devices in a mesh: wide: 64 (over y, z, core), narrow: 4 (over x).
Axes of the slice: x: 4, y: 4, z: 8, core: 2. Of those that a mesh axis runs over, the one named last changes fastest.
Arguments:
- upper_panel: float32 [15360, 1024], P('wide', 'narrow'), may hold values from -0.1875 to 0.1875
- coupling: float32 [512, 512], P('wide'), may hold values from -0.25 to 0.25
- diag_inverse: float32 [2, 512, 512], replicated, as said below
- block_rhs: float32 [2, 512, 2048], P(None, 'wide'), may hold values from -6 to 6
- upper_rhs: float32 [15360, 2048], P('wide', 'narrow'), may hold values from -6 to 6
Outputs:
- solved: float32 [2, 512, 2048], P(None, 'wide', 'narrow')
- updated: float32 [15360, 2048], P('wide', 'narrow')
The draws below stay inside these ranges and needn't reach their ends.
Inputs may be any that keep to these rules, and one draw needn't show every extreme that they name: Each diag_inverse[k] is upper triangular with a positive diagonal.
All inputs are finite; a program needn't handle non-finite values.
Results may differ from the reference program's by a relative error of at most 0.000088.
Values sent between devices are 32-bit elements; how exact they have to be, the bound alone decides.
No kernel may reach another device: no remote copies, remote signals or barrier semaphores. Data moves between devices by JAX's collectives and lax.ppermute only.
A program may use at most 64 MiB of HBM per device.

```python
import jax
import jax.numpy as jnp
from jax import lax

R = 2048
BS = 512
M = 15360


def draw_diag_inverse(key, part):
    key_diag, key_off = jax.random.split(key)
    diagonal = jax.random.uniform(key_diag, (2, BS), jnp.float32, 1.0, 2.0)
    offdiag = jax.random.normal(key_off, (2, BS, BS), jnp.float32) / jnp.sqrt(jnp.float32(BS))
    row_index = jnp.arange(BS)[:, None]
    col_index = jnp.arange(BS)[None, :]
    above = (row_index < col_index)[None, :, :]
    onto = (row_index == col_index)[None, :, :]
    return jnp.where(onto, diagonal[:, :, None], jnp.where(above, offdiag, 0.0)).astype(jnp.float32)


def block_levels(stream_key, extent, cuts, smallest, high):
    level, own = 1.0, jax.random.fold_in(stream_key, 6)
    for axis_at, parts in cuts:
        steps = jnp.exp(jax.random.uniform(jax.random.fold_in(own, axis_at), (parts,), jnp.float32, smallest / len(cuts), high / len(cuts)))
        level = level * jnp.repeat(steps, extent[axis_at] // parts).reshape([-1 if axis == axis_at else 1 for axis in range(len(extent))])
    return level


def normal_values(own_key, extent, scale, bound, cuts=(), dtype=jnp.bfloat16):
    entries = scale * jax.random.normal(own_key, extent, jnp.float32)
    if cuts:
        entries = entries * block_levels(own_key, extent, cuts, -0.22, 0.18)
    return jnp.clip(entries, -bound, bound).astype(dtype)


def setup_inputs(seed: int = 0) -> dict:
    keys = jax.random.split(jax.random.key(seed), 6)
    return {
        "upper_panel": normal_values(keys[0], (M, 2 * BS), (2 * BS) ** -0.5, 0.1875, ((0, 64), (1, 4)), jnp.float32),
        "coupling": normal_values(keys[1], (BS, BS), BS ** -0.5, 0.25, ((0, 64),), jnp.float32),
        "diag_inverse": draw_diag_inverse(jax.random.fold_in(keys[5], 71), 0),
        "block_rhs": normal_values(keys[3], (2, BS, R), 1.0, 6.0, ((1, 64),), jnp.float32),
        "upper_rhs": normal_values(keys[4], (M, R), 1.0, 6.0, ((0, 64), (1, 4)), jnp.float32),
    }


def product(left, right):
    return jnp.dot(left, right, precision=lax.Precision.HIGHEST, preferred_element_type=jnp.float32)


def reference(upper_panel, coupling, diag_inverse, block_rhs, upper_rhs):
    last_block = product(diag_inverse[1], block_rhs[1])
    first_block = product(diag_inverse[0], block_rhs[0] - product(coupling, last_block))
    solved = jnp.stack([first_block, last_block])
    stacked = jnp.concatenate([first_block, last_block], axis=0)
    updated = upper_rhs - product(upper_panel, stacked)
    return solved, updated
```

```python
import jax
import jax.numpy as jnp
from jax import lax
from jax.sharding import PartitionSpec as P


Y, Z, CORES, X = 4, 8, 2, 4
PREC = lax.Precision.HIGHEST


def dot(left, right):
    return jnp.dot(left, right, precision=PREC, preferred_element_type=jnp.float32)


def index(y, z, c):
    return ((y % Y) * Z + z % Z) * CORES + c


def fetch(value, dy=0, dz=0, dc=0):
    pairs = [
        (index(y + dy, z + dz, c ^ dc), index(y, z, c))
        for y in range(Y)
        for z in range(Z)
        for c in range(CORES)
    ]
    return lax.ppermute(value, "wide", pairs)


def local(upper_panel, coupling, diag_inverse, block_rhs, upper_rhs):
    wide = lax.axis_index("wide")
    narrow = lax.axis_index("narrow")
    rows = block_rhs.shape[1]
    targets = upper_rhs.shape[1]
    half = diag_inverse.shape[1]
    y, z, core = wide // (Z * CORES), (wide // CORES) % Z, wide % CORES

    own = lax.dynamic_slice_in_dim(block_rhs, narrow * targets, targets, 2)
    mine = jnp.concatenate([own, coupling[None]], axis=0)

    up = fetch(mine, dz=1)
    down = fetch(mine, dz=-1)
    far = fetch(mine, dz=4)
    up2 = fetch(jnp.stack([mine, up]), dz=2)
    down2 = fetch(jnp.stack([mine, down]), dz=-2)
    ring = jnp.stack([mine, up, up2[0], up2[1], far, down2[1], down2[0], down])
    y1 = fetch(ring, dy=1)
    y3 = fetch(ring, dy=-1)
    y2 = fetch(ring, dy=2)
    same = jnp.stack([ring, y1, y2, y3])
    other = fetch(same, dc=1)

    panels = [upper_panel] + [
        lax.ppermute(upper_panel, "narrow", [((i + d) % X, i) for i in range(X)])
        for d in (1, 2, 3)
    ]
    panel = jnp.roll(jnp.stack(panels), narrow, axis=0)
    unit = jnp.where(
        jnp.arange(half)[None, :] == wide * rows + jnp.arange(rows)[:, None], -1.0, 0.0
    ).astype(jnp.float32)
    zero = jnp.zeros_like(unit)
    left0 = jnp.concatenate([jnp.concatenate([panel[0], panel[1]], 1), unit, zero], 0)
    left1 = jnp.concatenate([jnp.concatenate([panel[2], panel[3]], 1), zero, unit], 0)
    weight0 = dot(left0, diag_inverse[0])

    both = jnp.stack([jnp.where(core == 0, same, other), jnp.where(core == 0, other, same)])
    both = jnp.roll(both, (y, z), axis=(1, 2)).transpose(3, 1, 2, 0, 4, 5)
    both = both.reshape(3, half, targets)

    weight1 = dot(left1 - dot(weight0, both[2]), diag_inverse[1])
    product = dot(weight0, both[0]) + dot(weight1, both[1])
    count = upper_rhs.shape[0]
    updated = upper_rhs - product[:count]
    solved = -product[count:].reshape(2, rows, targets)
    return (solved, updated)


def solution(mesh):
    return jax.shard_map(
        local,
        mesh=mesh,
        in_specs=(
            P("wide", "narrow"),
            P("wide", None),
            P(),
            P(None, "wide", None),
            P("wide", "narrow"),
        ),
        out_specs=(P(None, "wide", "narrow"), P("wide", "narrow")),
        check_vma=False,
    )
```

```python
import jax
import jax.numpy as jnp
from jax import lax
from jax.experimental import pallas as pl
from jax.experimental.pallas import tpu as pltpu
from jax.sharding import PartitionSpec as P


Y, Z, CORES, X = 4, 8, 2, 4
ROUNDS = ((0, 1, 7, 2, 6), (3, 5, 4))
LANES = 128


def index(y, z, c):
    return ((y % Y) * Z + z % Z) * CORES + c


def fetch(value, dy=0, dz=0, dc=0):
    pairs = [
        (index(y + dy, z + dz, c ^ dc), index(y, z, c))
        for y in range(Y)
        for z in range(Z)
        for c in range(CORES)
    ]
    return lax.ppermute(value, "wide", pairs)


def split(value):
    high = value.astype(jnp.bfloat16)
    return high, (value - high.astype(jnp.float32)).astype(jnp.bfloat16)


def dot1(left, right):
    return jnp.dot(left, right, preferred_element_type=jnp.float32)


def dot3(left, right):
    return dot1(left[0], right[0]) + (dot1(left[0], right[1]) + dot1(left[1], right[0]))


def take_kernel(at, rhs, coupling, out, sems):
    targets = out.shape[2]
    where = pl.multiple_of(at[1] * targets, targets)
    kinds = rhs.shape[0]
    copies = [
        pltpu.make_async_copy(rhs.at[:, :, pl.ds(where, targets)], out.at[:kinds], sems.at[0]),
        pltpu.make_async_copy(coupling, out.at[kinds], sems.at[1]),
    ]
    for copy in copies:
        copy.start()
    for copy in copies:
        copy.wait()


def pair_kernel(own, near, out, sem):
    copy = pltpu.make_async_copy(own, out.at[0], sem)
    copy.start()
    out[1] = near[...]
    copy.wait()


def stack_kernel(*refs):
    for n, ref in enumerate(refs[:-1]):
        refs[-1][n] = ref[...]


def spans(rows):
    counts = [CORES * Y * len(r) * rows for r in ROUNDS]
    return [(n, -(-n // LANES) * LANES) for n in counts]


def arrival(wide, rows):
    y, z, core = wide >> 4, (wide >> 1) & (Z - 1), wide & 1
    parts = []
    for ring, (used, width) in zip(ROUNDS, spans(rows)):
        j = lax.broadcasted_iota(jnp.int32, (1, width), 1)
        piece, slot = jnp.zeros_like(j), j >> 3
        for n in range(1, CORES * Y):
            piece = jnp.where(slot >= n * len(ring), n, piece)
        slot = slot - piece * len(ring)
        rz = jnp.zeros_like(j)
        for n, offset in enumerate(ring):
            rz = jnp.where(slot == n, offset, rz)
        row = (y + (piece & (Y - 1))) & (Y - 1)
        block = (row * Z + ((z + rz) & (Z - 1))) * CORES + (core ^ (piece >> 2))
        parts.append(jnp.where(j < used, block * rows + (j & (rows - 1)), -1))
    return jnp.concatenate(parts, axis=1)


def weights_kernel(
    at, near, pair, p0, inverse, w0h, w0l, d1h, d1l, left1_ref, left, inv, sems
):
    count, width = p0.shape
    half = inverse.shape[1]
    total = left.shape[0]
    rows = (total - count) // 2
    own = pl.multiple_of(at[1] * width, width)
    copies = [
        pltpu.make_async_copy(p0, left.at[pl.ds(0, count), pl.ds(own, width)], sems.at[2]),
        pltpu.make_async_copy(inverse.at[0], inv.at[0], sems.at[0]),
        pltpu.make_async_copy(inverse.at[1], inv.at[1], sems.at[1]),
    ]
    for copy in copies:
        copy.start()
    for mask, piece in ((1, near), (3, pair.at[0]), (2, pair.at[1])):
        where = pl.multiple_of((at[1] ^ mask) * width, width)
        left[pl.ds(0, count), pl.ds(where, width)] = piece[...]
    row = lax.broadcasted_iota(jnp.int32, (rows, half), 0)
    col = lax.broadcasted_iota(jnp.int32, (rows, half), 1)
    unit = jnp.where(col == at[0] * rows + row, -1.0, 0.0).astype(jnp.float32)
    zero = jnp.zeros_like(unit)
    left[pl.ds(count, rows), pl.ds(0, half)] = unit
    left[pl.ds(count, rows), pl.ds(half, half)] = zero
    left[pl.ds(count + rows, rows), pl.ds(0, half)] = zero
    left[pl.ds(count + rows, rows), pl.ds(half, half)] = unit
    order = arrival(at[0], rows)
    natural = lax.broadcasted_iota(jnp.int32, (half, order.shape[1]), 0)
    choose = jnp.where(natural == order, 1.0, 0.0).astype(jnp.bfloat16)
    for copy in copies:
        copy.wait()
    w0 = split(dot3(split(left[:, :half]), split(inv[0])))
    d1 = split(inv[1])
    for ref, part in ((w0h, w0[0]), (w0l, w0[1]), (d1h, d1[0]), (d1l, d1[1])):
        ref[...] = dot1(part, choose).astype(jnp.bfloat16)
    left1_ref[...] = left[:, half:]


def gather_kinds(refs, scratch):
    for n, ref in enumerate(refs):
        blocks, _, rows, _ = ref.shape
        for b in range(blocks):
            for kind in range(3):
                scratch[kind, pl.ds((n * blocks + b) * rows, rows), :] = ref[b, kind]
    used = len(refs) * refs[0].shape[0] * refs[0].shape[2]
    if used < scratch.shape[1]:
        scratch[:, pl.ds(used, scratch.shape[1] - used), :] = jnp.zeros(
            (scratch.shape[0], scratch.shape[1] - used, scratch.shape[2]), jnp.float32
        )


def first_kernel(*refs):
    pieces, (w0h, w0l, left1, t_ref, acc_ref, b1h, b1l, scratch) = refs[:8], refs[8:]
    gather_kinds(pieces, scratch)
    cut = scratch.shape[1]
    w0 = w0h[:, :cut], w0l[:, :cut]
    t_ref[...] = left1[...] - dot3(w0, split(scratch[2]))
    acc_ref[...] = dot3(w0, split(scratch[0]))
    b1h[...], b1l[...] = split(scratch[1])


def last_kernel(*refs):
    pieces = refs[:8]
    w0h, w0l, d1h, d1l, t, acc, b1h, b1l, base, solved_ref, updated_ref, scratch = refs[8:]
    gather_kinds(pieces, scratch)
    cut = b1h.shape[0]
    w0 = w0h[:, cut:], w0l[:, cut:]
    w1 = dot3(split(t[...] - dot3(w0, split(scratch[2]))), (d1h[...], d1l[...]))
    out = (
        (acc[...] + dot3(w0, split(scratch[0])))
        + dot3(split(w1[:, :cut]), (b1h[...], b1l[...]))
        + dot3(split(w1[:, cut:]), split(scratch[1]))
    )
    count = base.shape[0]
    rows = solved_ref.shape[1]
    updated_ref[...] = base[...] - out[:count]
    solved_ref[0] = -out[count : count + rows]
    solved_ref[1] = -out[count + rows :]


def vmem(n):
    return [pl.BlockSpec(memory_space=pltpu.VMEM)] * n


def params(mib):
    return pltpu.CompilerParams(vmem_limit_bytes=mib << 20)


def cost(flops):
    return pl.CostEstimate(flops=flops, bytes_accessed=4 << 20, transcendentals=0)


def body(upper_panel, coupling, diag_inverse, block_rhs, upper_rhs):
    wide = lax.axis_index("wide")
    narrow = lax.axis_index("narrow")
    rows = block_rhs.shape[1]
    count, targets = upper_rhs.shape
    half = diag_inverse.shape[1]
    total = count + 2 * rows
    f32 = jnp.float32

    at = jnp.stack([wide, narrow]).astype(jnp.int32)
    block_rhs, coupling, upper_panel_hbm, diag_inverse = (
        pltpu.with_memory_space_constraint(a, pltpu.HBM)
        for a in (block_rhs, coupling, upper_panel, diag_inverse)
    )
    smem = [pl.BlockSpec(memory_space=pltpu.SMEM)]
    hbm = pl.BlockSpec(memory_space=pltpu.HBM)
    unit = (3, rows, targets)
    ring = {
        0: pl.pallas_call(
            take_kernel,
            out_shape=jax.ShapeDtypeStruct(unit, f32),
            in_specs=smem + [hbm] * 2,
            out_specs=vmem(1)[0],
            scratch_shapes=[pltpu.SemaphoreType.DMA((2,))],
            compiler_params=params(4),
            name="take",
        )(at, block_rhs, coupling)
    }
    ring[1] = fetch(ring[0], dz=1)
    ring[7] = fetch(ring[0], dz=-1)
    ring[2] = fetch(ring[1], dz=1)
    ring[6] = fetch(ring[7], dz=-1)
    ring[3] = fetch(ring[1], dz=2)
    ring[5] = fetch(ring[7], dz=-2)
    ring[4] = fetch(ring[2], dz=2)

    def from_narrow(value, mask):
        return lax.ppermute(value, "narrow", [(i ^ mask, i) for i in range(X)])

    near = from_narrow(upper_panel, 1)
    both = pl.pallas_call(
        pair_kernel,
        out_shape=jax.ShapeDtypeStruct((2,) + upper_panel.shape, f32),
        in_specs=[hbm] + vmem(1),
        out_specs=vmem(1)[0],
        scratch_shapes=[pltpu.SemaphoreType.DMA],
        compiler_params=params(4),
        name="pair",
    )(upper_panel_hbm, near)
    pair = from_narrow(both, 3)

    gathered = []
    for n, offsets in enumerate(ROUNDS):
        mine = pl.pallas_call(
            stack_kernel,
            out_shape=jax.ShapeDtypeStruct((len(offsets),) + unit, f32),
            in_specs=vmem(len(offsets)),
            out_specs=vmem(1)[0],
            compiler_params=params(4),
        )(*[ring[o] for o in offsets])
        y1 = fetch(mine, dy=1)
        y3 = fetch(mine, dy=-1)
        y2 = fetch(y1, dy=1) if n == 0 else fetch(y3, dy=-1)
        same = [mine, y1, y2, y3]
        other = [fetch(s, dc=1) for s in same]
        gathered.append(same + other)

    flops = 2 * total * half * half
    bf16 = jnp.bfloat16
    cut, rest = (width for _, width in spans(rows))
    packed = cut + rest
    w0h, w0l, d1h, d1l, left1 = pl.pallas_call(
        weights_kernel,
        out_shape=[
            jax.ShapeDtypeStruct((total, packed), bf16),
            jax.ShapeDtypeStruct((total, packed), bf16),
            jax.ShapeDtypeStruct((half, packed), bf16),
            jax.ShapeDtypeStruct((half, packed), bf16),
            jax.ShapeDtypeStruct((total, half), f32),
        ],
        in_specs=smem + vmem(2) + [hbm] * 2,
        out_specs=vmem(5),
        scratch_shapes=[
            pltpu.VMEM((total, 2 * half), f32),
            pltpu.VMEM((2, half, half), f32),
            pltpu.SemaphoreType.DMA((3,)),
        ],
        cost_estimate=cost(4 * flops),
        compiler_params=params(14),
        name="weights",
    )(at, near, pair, upper_panel_hbm, diag_inverse)
    t, acc, b1h, b1l = pl.pallas_call(
        first_kernel,
        out_shape=[
            jax.ShapeDtypeStruct((total, half), f32),
            jax.ShapeDtypeStruct((total, targets), f32),
            jax.ShapeDtypeStruct((cut, targets), bf16),
            jax.ShapeDtypeStruct((cut, targets), bf16),
        ],
        in_specs=vmem(11),
        out_specs=vmem(4),
        scratch_shapes=[pltpu.VMEM((3, cut, targets), f32)],
        cost_estimate=cost(flops),
        compiler_params=params(10),
        name="first",
    )(*gathered[0], w0h, w0l, left1)
    solved, updated = pl.pallas_call(
        last_kernel,
        out_shape=[
            jax.ShapeDtypeStruct((2, rows, targets), f32),
            jax.ShapeDtypeStruct((count, targets), f32),
        ],
        in_specs=vmem(17),
        out_specs=vmem(2),
        scratch_shapes=[pltpu.VMEM((3, rest, targets), f32)],
        cost_estimate=cost(3 * flops),
        compiler_params=params(12),
        name="last",
    )(*gathered[1], w0h, w0l, d1h, d1l, t, acc, b1h, b1l, upper_rhs)
    return (solved, updated)


def solution(mesh):
    return jax.shard_map(
        body,
        mesh=mesh,
        in_specs=(
            P("wide", "narrow"),
            P("wide", None),
            P(),
            P(None, "wide", None),
            P("wide", "narrow"),
        ),
        out_specs=(P(None, "wide", "narrow"), P("wide", "narrow")),
        check_vma=False,
    )
```

```python
import jax
import jax.numpy as jnp
from jax import lax
from jax.experimental import pallas as pl
from jax.experimental.pallas import tpu as pltpu
from jax.sharding import PartitionSpec as P


Y, Z, CORES, X = 4, 8, 2, 4
ROUNDS = ((0, 1, 7, 2, 6, 3), (5, 4))


def index(y, z, c):
    return ((y % Y) * Z + z % Z) * CORES + c


def fetch(value, dy=0, dz=0, dc=0):
    pairs = [
        (index(y + dy, z + dz, c ^ dc), index(y, z, c))
        for y in range(Y)
        for z in range(Z)
        for c in range(CORES)
    ]
    return lax.ppermute(value, "wide", pairs)


def split(value):
    high = value.astype(jnp.bfloat16)
    return high, (value - high.astype(jnp.float32)).astype(jnp.bfloat16)


def dot1(left, right):
    return jnp.dot(left, right, preferred_element_type=jnp.float32)


def dot3(left, right):
    return dot1(left[0], right[0]) + (dot1(left[0], right[1]) + dot1(left[1], right[0]))


def run(copies):
    for copy in copies:
        copy.start()
    for copy in copies:
        copy.wait()


def take_kernel(rhs, coupling, out, sems):
    targets = out.shape[2]
    where = pl.multiple_of(lax.axis_index("narrow") * targets, targets)
    kinds = rhs.shape[0]
    run(
        [
            pltpu.make_async_copy(
                rhs.at[:, :, pl.ds(where, targets)], out.at[:kinds], sems.at[0]
            ),
            pltpu.make_async_copy(coupling, out.at[kinds], sems.at[1]),
        ]
    )


def load_kernel(inverse, panel, inv, own, sems):
    half = inverse.shape[1]
    mid = half // 2
    low = pl.ds(mid, half - mid)
    run(
        [
            pltpu.make_async_copy(panel, own, sems.at[0]),
            pltpu.make_async_copy(inverse.at[:, :mid], inv.at[:, :mid], sems.at[1]),
            pltpu.make_async_copy(inverse.at[:, low, low], inv.at[:, low, low], sems.at[2]),
        ]
    )


def stack_kernel(*refs):
    for n, ref in enumerate(refs[:-1]):
        refs[-1][n] = ref[...]


def arrival(wide, rows, half):
    y, z, core = wide >> 4, (wide >> 1) & (Z - 1), wide & 1
    j = lax.broadcasted_iota(jnp.int32, (1, half), 1)
    cell = j // rows
    piece, rz = jnp.zeros_like(j), jnp.zeros_like(j)
    start = 0
    for ring in ROUNDS:
        for n in range(CORES * Y):
            for offset in ring:
                piece = jnp.where(cell == start, n, piece)
                rz = jnp.where(cell == start, offset, rz)
                start += 1
    row = (y + (piece & (Y - 1))) & (Y - 1)
    block = (row * Z + ((z + rz) & (Z - 1))) * CORES + (core ^ (piece >> 2))
    return block * rows + (j & (rows - 1))


def weights_kernel(own, p1, p2, p3, inv, w0h, w0l, d1h, d1l, left1_ref, left):
    count, width = own.shape
    half = inv.shape[1]
    mid = half // 2
    total = left.shape[0]
    rows = (total - count) // 2
    wide, narrow = lax.axis_index("wide"), lax.axis_index("narrow")
    for step, piece in enumerate((own, p1, p2, p3)):
        where = pl.multiple_of(((narrow + step) & (X - 1)) * width, width)
        left[pl.ds(0, count), pl.ds(where, width)] = piece[...]
    row = lax.broadcasted_iota(jnp.int32, (rows, half), 0)
    col = lax.broadcasted_iota(jnp.int32, (rows, half), 1)
    unit = jnp.where(col == wide * rows + row, -1.0, 0.0).astype(jnp.float32)
    zero = jnp.zeros_like(unit)
    left[pl.ds(count, rows), pl.ds(0, half)] = unit
    left[pl.ds(count, rows), pl.ds(half, half)] = zero
    left[pl.ds(count + rows, rows), pl.ds(0, half)] = zero
    left[pl.ds(count + rows, rows), pl.ds(half, half)] = unit
    order = arrival(wide, rows, half)
    natural = lax.broadcasted_iota(jnp.int32, (half, half), 0)
    choose = jnp.where(natural == order, 1.0, 0.0).astype(jnp.bfloat16)
    left0 = split(left[:, :half])
    w0 = [
        dot3([p[:, :mid] for p in left0], split(inv[0, :mid, :mid])),
        dot3(left0, split(jnp.concatenate([inv[0, :mid, mid:], inv[0, mid:, mid:]], 0))),
    ]
    w0 = split(jnp.concatenate(w0, 1))
    for ref, part in ((w0h, w0[0]), (w0l, w0[1])):
        ref[...] = dot1(part, choose).astype(jnp.bfloat16)
    for ref, top, low in zip((d1h, d1l), split(inv[1, :mid]), split(inv[1, mid:, mid:])):
        ref[:mid] = dot1(top, choose).astype(jnp.bfloat16)
        ref[mid:] = dot1(low, choose[mid:]).astype(jnp.bfloat16)
    left1_ref[...] = left[:, half:]


def gather_kinds(refs, scratch, at):
    kinds, height, targets = scratch.shape
    first = at
    for ref in refs:
        for b in range(ref.shape[0]):
            for kind in range(kinds):
                scratch[kind, pl.ds(at, ref.shape[2]), :] = ref[b, kind]
            at += ref.shape[2]
    for low, high in ((0, first), (at, height)):
        if low < high:
            scratch[:, pl.ds(low, high - low), :] = jnp.zeros(
                (kinds, high - low, targets), jnp.float32
            )


def first_kernel(*refs):
    pieces, (w0h, w0l, left1, t_ref, acc_ref, b1h, b1l, scratch) = refs[:8], refs[8:]
    gather_kinds(pieces, scratch, 0)
    height = scratch.shape[1]
    w0 = w0h[:, :height], w0l[:, :height]
    t_ref[...] = left1[...] - dot3(w0, split(scratch[2]))
    acc_ref[...] = dot3(w0, split(scratch[0]))
    b1h[...], b1l[...] = split(scratch[1, : b1h.shape[0]])


def last_kernel(*refs):
    pieces = refs[:8]
    w0h, w0l, d1h, d1l, t, acc, b1h, b1l, base, solved_ref, updated_ref, scratch, whole = refs[8:]
    height = scratch.shape[1]
    done = b1h.shape[0]
    half = whole.shape[1]
    left = half - done
    gather_kinds(pieces, scratch, height - left)
    w0 = w0h[:, half - height :], w0l[:, half - height :]
    inner = split(t[...] - dot3(w0, split(scratch[2])))
    for n, (ref, part) in enumerate(zip((b1h, b1l), split(scratch[1, height - left :]))):
        whole[n, :done] = ref[...]
        whole[n, done:] = part
    w1 = split(dot3(inner, (d1h[...], d1l[...])))
    out = (acc[...] + dot3(w0, split(scratch[0]))) + dot3(w1, (whole[0], whole[1]))
    count = base.shape[0]
    rows = solved_ref.shape[1]
    updated_ref[...] = base[...] - out[:count]
    solved_ref[0] = -out[count : count + rows]
    solved_ref[1] = -out[count + rows :]


def vmem(n):
    return [pl.BlockSpec(memory_space=pltpu.VMEM)] * n


def params(mib):
    return pltpu.CompilerParams(vmem_limit_bytes=mib << 20)


def cost(flops):
    return pl.CostEstimate(flops=flops, bytes_accessed=4 << 20, transcendentals=0)


def body(upper_panel, coupling, diag_inverse, block_rhs, upper_rhs):
    rows = block_rhs.shape[1]
    count, targets = upper_rhs.shape
    half = diag_inverse.shape[1]
    total = count + 2 * rows
    f32 = jnp.float32

    block_rhs, coupling, upper_panel_hbm, diag_inverse = (
        pltpu.with_memory_space_constraint(a, pltpu.HBM)
        for a in (block_rhs, coupling, upper_panel, diag_inverse)
    )
    hbm = pl.BlockSpec(memory_space=pltpu.HBM)
    unit = (3, rows, targets)
    ring = {
        0: pl.pallas_call(
            take_kernel,
            out_shape=jax.ShapeDtypeStruct(unit, f32),
            in_specs=[hbm] * 2,
            out_specs=vmem(1)[0],
            scratch_shapes=[pltpu.SemaphoreType.DMA((2,))],
            compiler_params=params(4),
            name="take",
        )(block_rhs, coupling)
    }
    inverses, panel = pl.pallas_call(
        load_kernel,
        out_shape=[
            jax.ShapeDtypeStruct(diag_inverse.shape, f32),
            jax.ShapeDtypeStruct(upper_panel.shape, f32),
        ],
        in_specs=[hbm] * 2,
        out_specs=vmem(2),
        scratch_shapes=[pltpu.SemaphoreType.DMA((3,))],
        compiler_params=params(6),
        name="load",
    )(diag_inverse, upper_panel_hbm)
    ring[1] = fetch(ring[0], dz=1)
    ring[7] = fetch(ring[0], dz=-1)
    ring[2] = fetch(ring[1], dz=1)
    ring[6] = fetch(ring[7], dz=-1)
    ring[3] = fetch(ring[1], dz=2)
    ring[5] = fetch(ring[7], dz=-2)
    ring[4] = fetch(ring[2], dz=2)

    def from_narrow(value, d):
        return lax.ppermute(value, "narrow", [((i + d) % X, i) for i in range(X)])

    panel1 = from_narrow(upper_panel, 1)
    panel3 = from_narrow(upper_panel, -1)
    panel2 = from_narrow(panel1, 1)

    gathered = []
    for n, offsets in enumerate(ROUNDS):
        mine = pl.pallas_call(
            stack_kernel,
            out_shape=jax.ShapeDtypeStruct((len(offsets),) + unit, f32),
            in_specs=vmem(len(offsets)),
            out_specs=vmem(1)[0],
            compiler_params=params(4),
        )(*[ring[o] for o in offsets])
        y1 = fetch(mine, dy=1)
        y3 = fetch(mine, dy=-1)
        y2 = fetch(y1, dy=1) if n == 0 else fetch(y3, dy=-1)
        same = [mine, y1, y2, y3]
        other = [fetch(s, dc=1) for s in same]
        gathered.append(same + other)

    flops = 2 * total * half * half
    bf16 = jnp.bfloat16
    done = CORES * Y * len(ROUNDS[0]) * rows
    cut, rest = -(-done // 128) * 128, -(-(half - done) // 128) * 128
    w0h, w0l, d1h, d1l, left1 = pl.pallas_call(
        weights_kernel,
        out_shape=[
            jax.ShapeDtypeStruct((total, half), bf16),
            jax.ShapeDtypeStruct((total, half), bf16),
            jax.ShapeDtypeStruct((half, half), bf16),
            jax.ShapeDtypeStruct((half, half), bf16),
            jax.ShapeDtypeStruct((total, half), f32),
        ],
        in_specs=vmem(5),
        out_specs=vmem(5),
        scratch_shapes=[
            pltpu.VMEM((total, 2 * half), f32),
        ],
        cost_estimate=cost(4 * flops),
        compiler_params=params(14),
        name="weights",
    )(panel, panel1, panel2, panel3, inverses)
    t, acc, b1h, b1l = pl.pallas_call(
        first_kernel,
        out_shape=[
            jax.ShapeDtypeStruct((total, half), f32),
            jax.ShapeDtypeStruct((total, targets), f32),
            jax.ShapeDtypeStruct((done, targets), bf16),
            jax.ShapeDtypeStruct((done, targets), bf16),
        ],
        in_specs=vmem(11),
        out_specs=vmem(4),
        scratch_shapes=[pltpu.VMEM((3, cut, targets), f32)],
        cost_estimate=cost(flops),
        compiler_params=params(10),
        name="first",
    )(*gathered[0], w0h, w0l, left1)
    solved, updated = pl.pallas_call(
        last_kernel,
        out_shape=[
            jax.ShapeDtypeStruct((2, rows, targets), f32),
            jax.ShapeDtypeStruct((count, targets), f32),
        ],
        in_specs=vmem(17),
        out_specs=vmem(2),
        scratch_shapes=[pltpu.VMEM((3, rest, targets), f32), pltpu.VMEM((2, half, targets), bf16)],
        cost_estimate=cost(3 * flops),
        compiler_params=params(12),
        name="last",
    )(*gathered[1], w0h, w0l, d1h, d1l, t, acc, b1h, b1l, upper_rhs)
    return (solved, updated)


def solution(mesh):
    return jax.shard_map(
        body,
        mesh=mesh,
        in_specs=(
            P("wide", "narrow"),
            P("wide", None),
            P(),
            P(None, "wide", None),
            P("wide", "narrow"),
        ),
        out_specs=(P(None, "wide", "narrow"), P("wide", "narrow")),
        check_vma=False,
    )
```

```python
import jax
import jax.numpy as jnp
from jax import lax
from jax.experimental import pallas as pl
from jax.experimental.pallas import tpu as pltpu
from jax.sharding import PartitionSpec as P


Y, Z, CORES, X = 4, 8, 2, 4
ROUNDS = ((0, 1, 7, 2, 6, 3), (5, 4))


def index(y, z, c):
    return ((y % Y) * Z + z % Z) * CORES + c


def fetch(value, dy=0, dz=0, dc=0):
    pairs = [
        (index(y + dy, z + dz, c ^ dc), index(y, z, c))
        for y in range(Y)
        for z in range(Z)
        for c in range(CORES)
    ]
    return lax.ppermute(value, "wide", pairs)


def split(value):
    high = value.astype(jnp.bfloat16)
    return high, (value - high.astype(jnp.float32)).astype(jnp.bfloat16)


def dot1(left, right):
    return jnp.dot(left, right, preferred_element_type=jnp.float32)


def dot3(left, right):
    return dot1(left[0], right[0]) + (dot1(left[0], right[1]) + dot1(left[1], right[0]))


def run(copies):
    for copy in copies:
        copy.start()
    for copy in copies:
        copy.wait()


def take_kernel(rhs, coupling, out, sems):
    targets = out.shape[2]
    where = pl.multiple_of(lax.axis_index("narrow") * targets, targets)
    kinds = rhs.shape[0]
    run(
        [
            pltpu.make_async_copy(
                rhs.at[:, :, pl.ds(where, targets)], out.at[:kinds], sems.at[0]
            ),
            pltpu.make_async_copy(coupling, out.at[kinds], sems.at[1]),
        ]
    )


def load_kernel(inverse, panel, inv, own, sems):
    half = inverse.shape[1]
    mid = half // 2
    low = pl.ds(mid, half - mid)
    run(
        [
            pltpu.make_async_copy(panel, own, sems.at[0]),
            pltpu.make_async_copy(inverse.at[:, :mid], inv.at[:, :mid], sems.at[1]),
            pltpu.make_async_copy(inverse.at[:, low, low], inv.at[:, low, low], sems.at[2]),
        ]
    )


def stack_kernel(*refs):
    for n, ref in enumerate(refs[:-1]):
        refs[-1][n] = ref[...]


def arrival(wide, rows, half):
    y, z, core = wide >> 4, (wide >> 1) & (Z - 1), wide & 1
    j = lax.broadcasted_iota(jnp.int32, (1, half), 1)
    cell = j // rows
    piece, rz = jnp.zeros_like(j), jnp.zeros_like(j)
    start = 0
    for ring in ROUNDS:
        for n in range(CORES * Y):
            for offset in ring:
                piece = jnp.where(cell == start, n, piece)
                rz = jnp.where(cell == start, offset, rz)
                start += 1
    row = (y + (piece & (Y - 1))) & (Y - 1)
    block = (row * Z + ((z + rz) & (Z - 1))) * CORES + (core ^ (piece >> 2))
    return block * rows + (j & (rows - 1))


def weights_kernel(own, p1, p2, p3, inv, w0h, w0l, d1h, d1l, left1_ref, left):
    count, width = own.shape
    half = inv.shape[1]
    mid = half // 2
    total = left.shape[0]
    rows = (total - count) // 2
    wide, narrow = lax.axis_index("wide"), lax.axis_index("narrow")
    for step, piece in enumerate((own, p1, p2, p3)):
        where = pl.multiple_of(((narrow + step) & (X - 1)) * width, width)
        left[pl.ds(0, count), pl.ds(where, width)] = piece[...]
    row = lax.broadcasted_iota(jnp.int32, (rows, half), 0)
    col = lax.broadcasted_iota(jnp.int32, (rows, half), 1)
    unit = jnp.where(col == wide * rows + row, -1.0, 0.0).astype(jnp.float32)
    zero = jnp.zeros_like(unit)
    left[pl.ds(count, rows), pl.ds(0, half)] = unit
    left[pl.ds(count, rows), pl.ds(half, half)] = zero
    left[pl.ds(count + rows, rows), pl.ds(0, half)] = zero
    left[pl.ds(count + rows, rows), pl.ds(half, half)] = unit
    order = arrival(wide, rows, half)
    natural = lax.broadcasted_iota(jnp.int32, (half, half), 0)
    choose = jnp.where(natural == order, 1.0, 0.0).astype(jnp.bfloat16)
    left0 = split(left[:, :half])
    w0 = [
        dot3([p[:, :mid] for p in left0], split(inv[0, :mid, :mid])),
        dot3(left0, split(jnp.concatenate([inv[0, :mid, mid:], inv[0, mid:, mid:]], 0))),
    ]
    w0 = split(jnp.concatenate(w0, 1))
    for ref, part in ((w0h, w0[0]), (w0l, w0[1])):
        ref[...] = dot1(part, choose).astype(jnp.bfloat16)
    for ref, top, low in zip((d1h, d1l), split(inv[1, :mid]), split(inv[1, mid:, mid:])):
        ref[:mid] = dot1(top, choose).astype(jnp.bfloat16)
        ref[mid:] = dot1(low, choose[mid:]).astype(jnp.bfloat16)
    left1_ref[...] = left[:, half:]


def gather_parts(refs, high, low):
    at = 0
    for ref in refs:
        rows = 2 * ref.shape[2]
        for b in range(0, ref.shape[0], 2):
            for kind in range(ref.shape[1]):
                parts = split(jnp.concatenate([ref[b, kind], ref[b + 1, kind]], 0))
                high[kind, pl.ds(at, rows), :], low[kind, pl.ds(at, rows), :] = parts
            at += rows


def first_kernel(*refs):
    pieces, (w0h, w0l, left1, t_ref, acc_ref, b1h, b1l, high, low) = refs[:8], refs[8:]
    gather_parts(pieces, high, low)
    height = high.shape[1]
    w0 = w0h[:, :height], w0l[:, :height]
    t_ref[...] = left1[...] - dot3(w0, (high[2], low[2]))
    acc_ref[...] = dot3(w0, (high[0], low[0]))
    b1h[...], b1l[...] = high[1], low[1]


def last_kernel(*refs):
    pieces = refs[:8]
    w0h, w0l, d1h, d1l, t, acc, b1h, b1l, base, solved_ref, updated_ref, high, low, whole = refs[8:]
    done = b1h.shape[0]
    gather_parts(pieces, high, low)
    w0 = w0h[:, done:], w0l[:, done:]
    for n, (ref, part) in enumerate(((b1h, high), (b1l, low))):
        whole[n, :done], whole[n, done:] = ref[...], part[1]
    w1 = split(dot3(split(t[...] - dot3(w0, (high[2], low[2]))), (d1h[...], d1l[...])))
    out = (acc[...] + dot3(w0, (high[0], low[0]))) + dot3(w1, (whole[0], whole[1]))
    count = base.shape[0]
    rows = solved_ref.shape[1]
    updated_ref[...] = base[...] - out[:count]
    solved_ref[0] = -out[count : count + rows]
    solved_ref[1] = -out[count + rows :]


def vmem(n):
    return [pl.BlockSpec(memory_space=pltpu.VMEM)] * n


def params(mib):
    return pltpu.CompilerParams(vmem_limit_bytes=mib << 20)


def cost(flops):
    return pl.CostEstimate(flops=flops, bytes_accessed=4 << 20, transcendentals=0)


def body(upper_panel, coupling, diag_inverse, block_rhs, upper_rhs):
    rows = block_rhs.shape[1]
    count, targets = upper_rhs.shape
    half = diag_inverse.shape[1]
    total = count + 2 * rows
    f32 = jnp.float32

    block_rhs, coupling, upper_panel_hbm, diag_inverse = (
        pltpu.with_memory_space_constraint(a, pltpu.HBM)
        for a in (block_rhs, coupling, upper_panel, diag_inverse)
    )
    hbm = pl.BlockSpec(memory_space=pltpu.HBM)
    unit = (3, rows, targets)
    ring = {
        0: pl.pallas_call(
            take_kernel,
            out_shape=jax.ShapeDtypeStruct(unit, f32),
            in_specs=[hbm] * 2,
            out_specs=vmem(1)[0],
            scratch_shapes=[pltpu.SemaphoreType.DMA((2,))],
            compiler_params=params(4),
            name="take",
        )(block_rhs, coupling)
    }
    inverses, panel = pl.pallas_call(
        load_kernel,
        out_shape=[
            jax.ShapeDtypeStruct(diag_inverse.shape, f32),
            jax.ShapeDtypeStruct(upper_panel.shape, f32),
        ],
        in_specs=[hbm] * 2,
        out_specs=vmem(2),
        scratch_shapes=[pltpu.SemaphoreType.DMA((3,))],
        compiler_params=params(6),
        name="load",
    )(diag_inverse, upper_panel_hbm)
    ring[1] = fetch(ring[0], dz=1)
    ring[7] = fetch(ring[0], dz=-1)
    ring[2] = fetch(ring[1], dz=1)
    ring[6] = fetch(ring[7], dz=-1)
    ring[3] = fetch(ring[1], dz=2)
    ring[5] = fetch(ring[7], dz=-2)
    ring[4] = fetch(ring[2], dz=2)

    def from_narrow(value, d):
        return lax.ppermute(value, "narrow", [((i + d) % X, i) for i in range(X)])

    panel1 = from_narrow(upper_panel, 1)
    panel3 = from_narrow(upper_panel, -1)
    panel2 = from_narrow(panel1, 1)

    gathered = []
    for n, offsets in enumerate(ROUNDS):
        mine = pl.pallas_call(
            stack_kernel,
            out_shape=jax.ShapeDtypeStruct((len(offsets),) + unit, f32),
            in_specs=vmem(len(offsets)),
            out_specs=vmem(1)[0],
            compiler_params=params(4),
        )(*[ring[o] for o in offsets])
        y1 = fetch(mine, dy=1)
        y3 = fetch(mine, dy=-1)
        y2 = fetch(y1, dy=1) if n == 0 else fetch(y3, dy=-1)
        same = [mine, y1, y2, y3]
        other = [fetch(s, dc=1) for s in same]
        gathered.append(same + other)

    flops = 2 * total * half * half
    bf16 = jnp.bfloat16
    done = CORES * Y * len(ROUNDS[0]) * rows
    w0h, w0l, d1h, d1l, left1 = pl.pallas_call(
        weights_kernel,
        out_shape=[
            jax.ShapeDtypeStruct((total, half), bf16),
            jax.ShapeDtypeStruct((total, half), bf16),
            jax.ShapeDtypeStruct((half, half), bf16),
            jax.ShapeDtypeStruct((half, half), bf16),
            jax.ShapeDtypeStruct((total, half), f32),
        ],
        in_specs=vmem(5),
        out_specs=vmem(5),
        scratch_shapes=[
            pltpu.VMEM((total, 2 * half), f32),
        ],
        cost_estimate=cost(4 * flops),
        compiler_params=params(14),
        name="weights",
    )(panel, panel1, panel2, panel3, inverses)
    t, acc, b1h, b1l = pl.pallas_call(
        first_kernel,
        out_shape=[
            jax.ShapeDtypeStruct((total, half), f32),
            jax.ShapeDtypeStruct((total, targets), f32),
            jax.ShapeDtypeStruct((done, targets), bf16),
            jax.ShapeDtypeStruct((done, targets), bf16),
        ],
        in_specs=vmem(11),
        out_specs=vmem(4),
        scratch_shapes=[pltpu.VMEM((3, done, targets), bf16)] * 2,
        cost_estimate=cost(flops),
        compiler_params=params(10),
        name="first",
    )(*gathered[0], w0h, w0l, left1)
    solved, updated = pl.pallas_call(
        last_kernel,
        out_shape=[
            jax.ShapeDtypeStruct((2, rows, targets), f32),
            jax.ShapeDtypeStruct((count, targets), f32),
        ],
        in_specs=vmem(17),
        out_specs=vmem(2),
        scratch_shapes=[pltpu.VMEM((3, half - done, targets), bf16)] * 2
        + [pltpu.VMEM((2, half, targets), bf16)],
        cost_estimate=cost(3 * flops),
        compiler_params=params(12),
        name="last",
    )(*gathered[1], w0h, w0l, d1h, d1l, t, acc, b1h, b1l, upper_rhs)
    return (solved, updated)


def solution(mesh):
    return jax.shard_map(
        body,
        mesh=mesh,
        in_specs=(
            P("wide", "narrow"),
            P("wide", None),
            P(),
            P(None, "wide", None),
            P("wide", "narrow"),
        ),
        out_specs=(P(None, "wide", "narrow"), P("wide", "narrow")),
        check_vma=False,
    )
```
